32 devices in a mesh: seg: 4 (over z), sec: 8 (over y, x, core).
Axes of the slice: x: 2, y: 2, z: 4, core: 2. Of those that a mesh axis runs over, the one named last changes fastest.
Arguments:
- wave_first: float32 [4, 64, 128, 128], P('seg', 'sec')
- wave_second: float32 [4, 64, 128, 128], P('seg', 'sec')
- onsite_first: float32 [4, 64, 128, 128], P('seg', 'sec'), may hold values from 0.5 to 4
- onsite_second: float32 [4, 64, 128, 128], P('seg', 'sec'), may hold values from 0.5 to 4
- left_first: bfloat16 [4, 64, 16, 128, 128], P('seg', 'sec'), may hold values from -0.5 to 0.5
- right_first: bfloat16 [4, 64, 16, 128, 128], P('seg', 'sec'), may hold values from -0.125 to 0.125
- left_base: bfloat16 [4, 64, 16, 128, 128], P('seg', 'sec'), may hold values from -0.5 to 0.5
- right_second: bfloat16 [4, 64, 16, 128, 128], P('seg', 'sec'), may hold values from -0.125 to 0.125
- sources: int32 [64, 16], P('sec'), may hold values from 0 to 63, as said below
- block_dims: int32 [64], P('sec'), may hold values from 8 to 128, as said below
Outputs:
- result_first: float32 [4, 64, 128, 128], P('seg', 'sec')
- result_second: float32 [4, 64, 128, 128], P('seg', 'sec')
The draws below stay inside these ranges and needn't reach their ends.
Inputs may be any that keep to these rules, and one draw needn't show every extreme that they name: `sources`: each entry names a block whose index differs from its row's block by at most 8, and that difference is reached. `block_dims`: a multiple of 8.
All inputs are finite; a program needn't handle non-finite values.
Results may differ from the reference program's by a relative error of at most 0.015.
Values may be sent and summed in bfloat16 or wider, within the bound.
No kernel may reach another device: no remote copies, remote signals or barrier semaphores. Data moves between devices by JAX's collectives and lax.ppermute only.
A program may use at most 128 MiB of HBM per device.

```python
import math
import jax
import jax.numpy as jnp
from jax import lax

P_SIZE = 128
K = 16
STEPS = 3
BLK_DEV = 8
NBLK = 64
SEGS = 4


def wave_field(key):
    keys = jax.random.split(key, 3)
    shape = (SEGS, NBLK, P_SIZE, P_SIZE)
    base = jax.random.normal(keys[0], shape, jnp.float32)
    row_scale = jnp.exp(jax.random.uniform(keys[1], (SEGS, NBLK, P_SIZE, 1), jnp.float32, 0.0, math.log(10.0)))
    col_scale = jnp.exp(jax.random.uniform(keys[2], (SEGS, NBLK, 1, P_SIZE), jnp.float32, 0.0, math.log(10.0)))
    rising = 1.0 + 2.0 * jnp.arange(NBLK, dtype=jnp.float32) / max(NBLK - 1, 1)
    return 0.1 * base * row_scale * col_scale * rising[None, :, None, None]


def draw_wave_first(key, part):
    return wave_field(jax.random.fold_in(key, 11))


def draw_wave_second(key, part):
    return wave_field(jax.random.fold_in(key, 23))


def draw_sources(key, part):
    offsets = jax.random.randint(jax.random.fold_in(key, 37), (NBLK, K), -BLK_DEV, BLK_DEV + 1)
    column = jnp.arange(K, dtype=jnp.int32)[None, :]
    offsets = jnp.where(column == 0, BLK_DEV, jnp.where(column == 1, -BLK_DEV, offsets))
    target = jnp.arange(NBLK, dtype=jnp.int32)[:, None] + offsets
    return jnp.clip(target, 0, NBLK - 1).astype(jnp.int32)


def draw_block_dims(key, part):
    sizes = jax.random.randint(jax.random.fold_in(key, 41), (NBLK,), 1, P_SIZE // 8 + 1) * 8
    first = jnp.arange(NBLK, dtype=jnp.int32) == 0
    return jnp.where(first, P_SIZE, sizes).astype(jnp.int32)


def steps_of(stream_key, extent, pieces, low, top_value):
    gain = 1.0
    for dim, blocks in pieces:
        heights = jax.random.uniform(jax.random.fold_in(jax.random.fold_in(stream_key, 6), dim), (blocks,), jnp.float32, low / len(pieces), top_value / len(pieces))
        gain = gain * jnp.repeat(jnp.exp(heights), extent[dim] // blocks).reshape((-1,) + (1,) * (len(extent) - 1 - dim))
    return gain


def bell_draw(rng, extent, scale, most, cuts=(), held_as=jnp.bfloat16):
    values = jax.random.normal(rng, extent, jnp.float32) * scale
    if len(cuts) > 0:
        values = steps_of(rng, extent, cuts, -0.22, 0.18) * values
    return jnp.clip(values, min=-most, max=most).astype(held_as)


def setup_inputs(seed: int = 0) -> dict:
    arg_keys = jax.random.split(jax.random.key(seed), 11)
    return {
        "wave_first": draw_wave_first(jax.random.fold_in(arg_keys[10], 71), 0),
        "wave_second": draw_wave_second(jax.random.fold_in(arg_keys[10], 71), 0),
        "onsite_first": jnp.clip(jnp.exp(math.log(4.0) - 2.0794415 * jax.random.uniform(arg_keys[2], (SEGS, NBLK, P_SIZE, P_SIZE), jnp.float32) ** steps_of(arg_keys[2], (SEGS, NBLK, P_SIZE, P_SIZE), ((0, 4), (1, 8)), -0.2, 0.2)), 0.5, 4.0),
        "onsite_second": jnp.clip(jnp.exp(math.log(4.0) - 2.0794415 * jax.random.uniform(arg_keys[3], (SEGS, NBLK, P_SIZE, P_SIZE), jnp.float32) ** steps_of(arg_keys[3], (SEGS, NBLK, P_SIZE, P_SIZE), ((0, 4), (1, 8)), -0.2, 0.2)), 0.5, 4.0),
        "left_first": bell_draw(arg_keys[4], (SEGS, NBLK, K, P_SIZE, P_SIZE), P_SIZE ** -0.5, 0.5, ((0, 4), (1, 8))),
        "right_first": bell_draw(arg_keys[5], (SEGS, NBLK, K, P_SIZE, P_SIZE), (P_SIZE * K) ** -0.5, 0.125, ((0, 4), (1, 8))),
        "left_base": bell_draw(arg_keys[6], (SEGS, NBLK, K, P_SIZE, P_SIZE), P_SIZE ** -0.5, 0.5, ((0, 4), (1, 8))),
        "right_second": bell_draw(arg_keys[7], (SEGS, NBLK, K, P_SIZE, P_SIZE), (P_SIZE * K) ** -0.5, 0.125, ((0, 4), (1, 8))),
        "sources": draw_sources(jax.random.fold_in(arg_keys[10], 71), 0),
        "block_dims": draw_block_dims(jax.random.fold_in(arg_keys[10], 71), 0),
    }


def live_mask(block_dims):
    row_index = lax.broadcasted_iota(jnp.int32, (block_dims.shape[0], P_SIZE, P_SIZE), 1)
    col_index = lax.broadcasted_iota(jnp.int32, (block_dims.shape[0], P_SIZE, P_SIZE), 2)
    limit = block_dims[:, None, None]
    return ((row_index < limit) & (col_index < limit)).astype(jnp.float32)

def operate(vector, onsite, live, left_env, right_env, sources):
    packed = vector.astype(jnp.bfloat16)
    picked = packed[sources].astype(jnp.float32)
    left_part = jnp.einsum('bkij,bkjl->bkil', left_env.astype(jnp.float32), picked).astype(jnp.bfloat16)
    terms = jnp.einsum('bkil,bklm->bim', left_part.astype(jnp.float32), right_env.astype(jnp.float32))
    return live * (onsite * vector + terms)

def davidson(start, onsite, left_env, right_env, live, sources):
    vector = live * start
    for iteration in range(STEPS):
        image = operate(vector, onsite, live, left_env, right_env, sources)
        quotient = jnp.sum(vector * image) / jnp.sum(vector * vector)
        change = (image - quotient * vector) / (onsite + 1.0)
        moved = vector - change
        vector = moved / jnp.sqrt(jnp.sum(moved * moved) / (NBLK * P_SIZE * P_SIZE) + 1e-06)
    return vector

def build_left(pair):
    handed, base = pair
    handed_f = handed.astype(jnp.float32)
    carried = jnp.einsum('bkij,bjl->bkil', base.astype(jnp.float32), handed_f).astype(jnp.bfloat16)
    added = jnp.einsum('bji,bkjl->bkil', handed_f, carried.astype(jnp.float32))
    return (base.astype(jnp.float32) + added / P_SIZE).astype(jnp.bfloat16)

def reference(wave_first, wave_second, onsite_first, onsite_second, left_first, right_first, left_base, right_second, sources, block_dims):
    live = live_mask(block_dims)
    result_first = lax.map(lambda group: davidson(group[0], group[1], group[2], group[3], live, sources), (wave_first, onsite_first, left_first, right_first))
    handed = jnp.concatenate([jnp.zeros_like(result_first[:1]), result_first[:-1]], axis=0).astype(jnp.bfloat16)
    left_second = lax.map(build_left, (handed, left_base))
    result_second = lax.map(lambda group: davidson(group[0], group[1], group[2], group[3], live, sources), (wave_second, onsite_second, left_second, right_second))
    return (result_first, result_second)
```

```python
import functools

import jax
import jax.numpy as jnp
from jax import lax
from jax.experimental import pallas as pl
from jax.experimental.pallas import tpu as pltpu
from jax.sharding import PartitionSpec as P

STEPS = 3
EPS = 1e-6
F32 = jnp.float32
BF16 = jnp.bfloat16


def even_pairs(count):
    return [(i, i ^ 1) for i in range(count) if i ^ 1 < count]


def odd_pairs(count):
    pairs = [(i, i + 1 if i % 2 else i - 1) for i in range(1, count)]
    return [(i, j) for i, j in pairs if j < count]


def swapped(block):
    count = lax.axis_size("sec")
    odd = lax.ppermute(block, "sec", odd_pairs(count))
    even = lax.ppermute(block, "sec", even_pairs(count))
    return even, odd


def gathered_parts(partial):
    count = lax.axis_size("sec")
    if count & (count - 1) or count < 2:
        return [lax.psum(partial, "sec")]
    pair = partial + lax.ppermute(partial, "sec", even_pairs(count))
    others = [
        lax.ppermute(pair, "sec", [(i, i ^ (2 * m)) for i in range(count)])
        for m in range(1, count // 2)
    ]
    return [pair, *others]


def live_of(dim, width):
    rows = lax.broadcasted_iota(jnp.int32, (width, width), 0)
    cols = lax.broadcasted_iota(jnp.int32, (width, width), 1)
    return (rows < dim) & (cols < dim)


def folded(value):
    rows, lanes = value.shape
    return jnp.sum(value.reshape(rows // 8, 8, lanes), axis=0)


def put_row(ref, row, value):
    ref[row : row + 1, :] = jnp.sum(value, axis=0, keepdims=True)


def scalar_row(value, lanes):
    lane = lax.broadcasted_iota(jnp.int32, (1, lanes), 1)
    return jnp.where(lane == 0, value, 0.0)


def totals(refs):
    total = refs[0][...]
    for ref in refs[1:]:
        total = total + ref[...]
    return [jnp.sum(total[r : r + 1, :], axis=1, keepdims=True) for r in range(8)]


def apply_terms(src, dims, x, left, right, lxs, blocks, terms, width, emit):
    lanes = len(lxs)

    def body(i, carry):
        for j in range(lanes):
            b = i * lanes + j
            for k in range(terms):
                part = jnp.dot(left[b, k], x[src[b, k]], preferred_element_type=F32)
                lxs[j][:, k * width : (k + 1) * width] = part.astype(BF16)
            total = jnp.dot(
                lxs[j][...],
                right[b].reshape(terms * width, width),
                preferred_element_type=F32,
            )
            emit(b, jnp.where(live_of(dims[b], width), total, 0.0))
        return carry

    lax.fori_loop(0, blocks // lanes, body, 0)


def start_kernel(build, *refs):
    if build:
        src, dims, wave, onsite, even, odd, handed, base, right, *rest = refs
        u, term, sent, stats, left, x, acc, work, *lxs = rest
    else:
        src, dims, wave, onsite, even, odd, left, right, *rest = refs
        u, term, sent, stats, x, acc, *lxs = rest
    blocks, width = wave.shape[0], wave.shape[1]
    terms = left.shape[1]
    x[:blocks] = even[...]
    x[2 * blocks :] = odd[...]

    def first(b, carry):
        value = jnp.where(live_of(dims[b], width), wave[b], 0.0)
        u[b] = value
        x[blocks + b] = value.astype(BF16)
        return carry

    lax.fori_loop(0, blocks, first, 0)

    if build:

        def make(b, carry):
            block = handed[b]
            flipped = block.astype(F32).T.astype(BF16)
            carried = jnp.dot(
                base[b].reshape(terms * width, width), block, preferred_element_type=F32
            )
            work[...] = carried.astype(BF16)
            for k in range(terms):
                added = jnp.dot(
                    flipped, work[k * width : (k + 1) * width, :], preferred_element_type=F32
                )
                left[b, k] = (base[b, k].astype(F32) + added / width).astype(BF16)
            return carry

        lax.fori_loop(0, blocks, make, 0)

    acc[...] = jnp.zeros_like(acc)

    def emit(b, value):
        term[b] = value
        sent[b] = value.astype(BF16)
        mine = u[b]
        acc[0] += folded(mine * mine)
        acc[1] += folded(mine * (onsite[b] * mine + value))

    apply_terms(src, dims, x, left, right, lxs, blocks, terms, width, emit)
    stats[...] = jnp.zeros_like(stats)
    for row in range(2):
        put_row(stats, row, acc[row])


def next_kernel(n_parts, entries, share, first, last, *refs):
    src, dims, *rest = refs
    parts, rest = rest[:n_parts], rest[n_parts:]
    (u, term, onsite, left, right, u_even, u_odd, t_even, t_odd, w_even, w_odd, *rest) = rest
    if last:
        un, tn, stats, x, acc, *lxs = rest
    else:
        un, tn, sent, stats, un_even, un_odd, x, acc, *lxs = rest
    blocks, width = u.shape[0], u.shape[1]
    terms = left.shape[1]
    sums = totals(parts)
    quotient = sums[1] / sums[0]
    eps = EPS if first else sums[5]
    scale = 1.0 / jnp.sqrt(sums[0] / entries + eps)
    grow = (1.0 + quotient) * scale

    def others(w, before, t, after, at):
        def body(b, carry):
            value = w[b].astype(F32) * (
                grow * before[b].astype(F32) - scale * t[b].astype(F32)
            )
            if not last:
                after[b] = value
            x[at + b] = value.astype(BF16)
            return carry

        lax.fori_loop(0, blocks, body, 0)

    others(w_even, u_even, t_even, None if last else un_even, 0)
    others(w_odd, u_odd, t_odd, None if last else un_odd, 2 * blocks)

    def own(b, carry):
        value = (grow * u[b] - scale * term[b]) / (onsite[b] + 1.0)
        un[b] = value
        x[blocks + b] = value.astype(BF16)
        return carry

    lax.fori_loop(0, blocks, own, 0)
    acc[...] = jnp.zeros_like(acc)

    def emit(b, value):
        tn[b] = value
        mine = un[b]
        acc[0] += folded(mine * mine)
        acc[1] += folded(mine * (onsite[b] * mine + value))
        if last:
            weight = 1.0 / (onsite[b] + 1.0)
            along = weight * mine
            guess = (1.0 + quotient) * along - weight * value
            acc[2] += folded(guess * guess)
            acc[3] += folded(guess * along)
            acc[4] += folded(along * along)
        else:
            sent[b] = value.astype(BF16)

    apply_terms(src, dims, x, left, right, lxs, blocks, terms, width, emit)
    stats[...] = jnp.zeros_like(stats)
    for row in range(5 if last else 2):
        put_row(stats, row, acc[row])
    lanes = stats.shape[1]
    if last:
        stats[5:6, :] = scalar_row(quotient * share, lanes)
    else:
        stats[5:6, :] = scalar_row((EPS * scale * scale if first else EPS) * share, lanes)


def final_kernel(n_parts, entries, *refs):
    parts, rest = refs[:n_parts], refs[n_parts:]
    u, term, onsite, *outs = rest
    sums = totals(parts)
    quotient = sums[1] / sums[0]
    scale = 1.0 / jnp.sqrt(sums[0] / entries + EPS)
    delta = quotient - sums[5]
    length = sums[2] + 2.0 * delta * sums[3] + delta * delta * sums[4]
    scale = scale / jnp.sqrt(length * scale * scale / entries + EPS)
    grow = (1.0 + quotient) * scale

    def body(b, carry):
        value = (grow * u[b] - scale * term[b]) / (onsite[b] + 1.0)
        outs[0][b] = value
        if len(outs) > 1:
            outs[1][b] = value.astype(BF16)
        return carry

    lax.fori_loop(0, u.shape[0], body, 0)


VMEM = pl.BlockSpec(memory_space=pltpu.VMEM)
SMEM = pl.BlockSpec(memory_space=pltpu.SMEM)


def call(kernel, name, scalars, arrays, outs, scratch):
    return pl.pallas_call(
        kernel,
        name=name,
        out_shape=outs,
        in_specs=[SMEM] * len(scalars) + [VMEM] * len(arrays),
        out_specs=[VMEM] * len(outs),
        scratch_shapes=scratch,
        compiler_params=pltpu.CompilerParams(vmem_limit_bytes=24 << 20),
    )(*scalars, *arrays)


def like(shape, dtype):
    return jax.ShapeDtypeStruct(shape, dtype)


def on_device(*args):
    (
        wave_first,
        wave_second,
        onsite_first,
        onsite_second,
        left_first,
        right_first,
        left_base,
        right_second,
        sources,
        block_dims,
    ) = [a[0] if a.ndim > 3 else a for a in args]
    blocks, width = wave_first.shape[0], wave_first.shape[1]
    terms = left_first.shape[1]
    count = lax.axis_size("sec")
    entries = float(blocks * count * width * width)
    here = lax.axis_index("sec")
    local = sources - here * blocks + blocks
    group = local // blocks
    src = jnp.where(here % 2 == 0, (2 - group) * blocks + local % blocks, local)
    live = (jnp.arange(width)[None, :] < block_dims[:, None]).astype(F32)
    live = live[:, :, None] * live[:, None, :]

    lanes = max(j for j in (1, 2, 4) if blocks % j == 0)
    vec = (blocks, width, width)
    lxs = [pltpu.VMEM((width, terms * width), BF16)] * lanes
    xs = [pltpu.VMEM((3 * blocks, width, width), BF16), pltpu.VMEM((5, 8, width), F32)]
    stats_shape = like((8, width), F32)

    def update(wave, onsite, left, right, halo, w_halo, handed=None):
        build = handed is not None
        outs = [like(vec, F32), like(vec, F32), like(vec, BF16), stats_shape]
        ins = [wave, onsite, *halo]
        scratch = xs + lxs
        if build:
            ins += [handed]
            outs += [like(left.shape, BF16)]
            scratch = xs + [pltpu.VMEM((terms * width, width), BF16)] + lxs
        u, term, sent, stats, *built = call(
            functools.partial(start_kernel, build),
            "start_build" if build else "start",
            [src, block_dims],
            ins + [left, right],
            outs,
            scratch,
        )
        if build:
            (left,) = built
        u_halo = halo
        for step in range(1, STEPS):
            last = step == STEPS - 1
            t_halo = swapped(sent)
            parts = gathered_parts(stats)
            outs = [like(vec, F32), like(vec, F32)]
            if last:
                outs += [stats_shape]
            else:
                outs += [like(vec, BF16), stats_shape, like(vec, F32), like(vec, F32)]
            res = call(
                functools.partial(
                    next_kernel, len(parts), entries, 1.0 / count, step == 1, last
                ),
                f"next_{step}",
                [src, block_dims],
                [*parts, u, term, onsite, left, right, *u_halo, *t_halo, *w_halo],
                outs,
                xs + lxs,
            )
            if last:
                u, term, stats = res
            else:
                u, term, sent, stats, *u_halo = res
        return u, term, gathered_parts(stats)

    def final(u, term, parts, onsite, narrow):
        outs = [like(vec, F32)] + ([like(vec, BF16)] if narrow else [])
        return call(
            functools.partial(final_kernel, len(parts), entries),
            "final",
            [],
            [*parts, u, term, onsite],
            outs,
            [],
        )

    halo_first = swapped((live * wave_first).astype(BF16))
    w_first = swapped((1.0 / (onsite_first + 1.0)).astype(BF16))
    halo_second = swapped((live * wave_second).astype(BF16))
    w_second = swapped((1.0 / (onsite_second + 1.0)).astype(BF16))

    u, term, parts = update(
        wave_first, onsite_first, left_first, right_first, halo_first, w_first
    )
    result_first, handed = final(u, term, parts, onsite_first, True)
    segs = lax.axis_size("seg")
    handed = lax.ppermute(handed, "seg", [(s, s + 1) for s in range(segs - 1)])
    u, term, parts = update(
        wave_second, onsite_second, left_base, right_second, halo_second, w_second, handed
    )
    (result_second,) = final(u, term, parts, onsite_second, False)
    return result_first[None], result_second[None]


def solution(mesh):
    vector = P("seg", "sec", None, None)
    matrices = P("seg", "sec", None, None, None)
    placed = (vector,) * 4 + (matrices,) * 4 + (P("sec", None), P("sec"))
    return jax.shard_map(
        on_device,
        mesh=mesh,
        in_specs=placed,
        out_specs=(vector, vector),
        check_vma=False,
    )
```

```python
import functools

import jax
import jax.numpy as jnp
from jax import lax
from jax.experimental import pallas as pl
from jax.experimental.pallas import tpu as pltpu
from jax.sharding import PartitionSpec as P

STEPS = 3
EPS = 1e-6
F32 = jnp.float32
BF16 = jnp.bfloat16


def even_pairs(count):
    return [(i, i ^ 1) for i in range(count) if i ^ 1 < count]


def odd_pairs(count):
    pairs = [(i, i + 1 if i % 2 else i - 1) for i in range(1, count)]
    return [(i, j) for i, j in pairs if j < count]


def swapped(block):
    count = lax.axis_size("sec")
    odd = lax.ppermute(block, "sec", odd_pairs(count))
    even = lax.ppermute(block, "sec", even_pairs(count))
    return even, odd


def gathered_parts(partial):
    count = lax.axis_size("sec")
    if count & (count - 1) or count < 2:
        return [lax.psum(partial, "sec")]
    pair = partial + lax.ppermute(partial, "sec", even_pairs(count))
    parts = [pair]
    for m in range(1, count // 2):
        parts += [lax.ppermute(pair, "sec", [(i, i ^ (2 * m)) for i in range(count)])]
    return parts


def live_of(dim, width):
    rows = lax.broadcasted_iota(jnp.int32, (width, width), 0)
    cols = lax.broadcasted_iota(jnp.int32, (width, width), 1)
    return (rows < dim) & (cols < dim)


def folded(value):
    rows, lanes = value.shape
    return jnp.sum(value.reshape(rows // 8, 8, lanes), axis=0)


def put_row(ref, row, value):
    ref[row : row + 1, :] = jnp.sum(value, axis=0, keepdims=True)


def scalar_row(value, lanes):
    lane = lax.broadcasted_iota(jnp.int32, (1, lanes), 1)
    return jnp.where(lane == 0, value, 0.0)


def totals(refs):
    total = refs[0][...]
    for ref in refs[1:]:
        total = total + ref[...]
    return [jnp.sum(total[r : r + 1, :], axis=1, keepdims=True) for r in range(8)]


def apply_terms(src, dims, x, left, right, lxs, blocks, terms, width, emit, ready=None):
    lanes = len(lxs)

    def body(i, carry):
        if ready is not None:
            ready(i)
        for j in range(lanes):
            b = i * lanes + j
            for k in range(terms):
                part = jnp.dot(left[b, k], x[src[b, k]], preferred_element_type=F32)
                lxs[j][:, k * width : (k + 1) * width] = part.astype(BF16)
            total = jnp.dot(
                lxs[j][...],
                right[b].reshape(terms * width, width),
                preferred_element_type=F32,
            )
            emit(b, jnp.where(live_of(dims[b], width), total, 0.0))
        return carry

    lax.fori_loop(0, blocks // lanes, body, 0)


def prepare_kernel(dims, wave, u, packed, sems):
    blocks, width, _ = u.shape
    copies = [pltpu.make_async_copy(wave.at[b], u.at[b], sems.at[b]) for b in range(blocks)]
    for copy in copies:
        copy.start()
    for b in range(blocks):
        copies[b].wait()
        value = jnp.where(live_of(dims[b], width), u[b], 0.0)
        u[b] = value
        packed[b] = value.astype(BF16)


def send_kernel(dims, packed, onsite_hbm, later_hbm, wave_hbm, *rest):
    weight, bundle, onsite, later, wave, sems = rest
    del packed
    pairs = ((onsite_hbm, onsite), (wave_hbm, wave), (later_hbm, later))
    copies = [pltpu.make_async_copy(s, t, sems.at[i]) for i, (s, t) in enumerate(pairs)]
    for copy in copies:
        copy.start()
    blocks, width, _ = wave.shape
    copies[0].wait()

    def first(b, carry):
        weight[b] = (1.0 / (onsite[b] + 1.0)).astype(BF16)
        return carry

    lax.fori_loop(0, blocks, first, 0)
    copies[1].wait()
    copies[2].wait()

    def second(b, carry):
        bundle[b] = jnp.where(live_of(dims[b], width), wave[b], 0.0).astype(BF16)
        bundle[blocks + b] = (1.0 / (later[b] + 1.0)).astype(BF16)
        return carry

    lax.fori_loop(0, blocks, second, 0)


def start_kernel(src, dims, even, odd, u, onsite_hbm, left_hbm, right_hbm, *rest):
    term, sent, stats, onsite, left, right, x, acc, sems, *lxs = rest
    blocks, terms, width, _ = left.shape
    lanes = len(lxs)

    def copies_of(group):
        part = pl.ds(group * lanes, lanes)
        pairs = ((left_hbm, left), (right_hbm, right), (onsite_hbm, onsite))
        return [
            pltpu.make_async_copy(s.at[part], t.at[part], sems.at[i, group])
            for i, (s, t) in enumerate(pairs)
        ]

    for group in range(blocks // lanes):
        for copy in copies_of(group):
            copy.start()
    x[:blocks] = even[...]
    x[2 * blocks :] = odd[...]

    def first(b, carry):
        x[blocks + b] = u[b].astype(BF16)
        return carry

    lax.fori_loop(0, blocks, first, 0)
    acc[...] = jnp.zeros_like(acc)

    def emit(b, value):
        term[b] = value
        sent[b] = value.astype(BF16)
        mine = u[b]
        acc[0] += folded(mine * mine)
        acc[1] += folded(mine * (onsite[b] * mine + value))

    def ready(group):
        for copy in copies_of(group):
            copy.wait()

    apply_terms(src, dims, x, left, right, lxs, blocks, terms, width, emit, ready)
    stats[...] = jnp.zeros_like(stats)
    for row in range(2):
        put_row(stats, row, acc[row])


def ahead_kernel(src, dims, even, odd, wave, right, u, y, x):
    blocks, terms, width, _ = right.shape
    x[:blocks] = even[...]
    x[2 * blocks :] = odd[...]

    def first(b, carry):
        value = jnp.where(live_of(dims[b], width), wave[b], 0.0)
        u[b] = value
        x[blocks + b] = value.astype(BF16)
        return carry

    lax.fori_loop(0, blocks, first, 0)

    def body(b, carry):
        for k in range(terms):
            part = jnp.dot(x[src[b, k]], right[b, k], preferred_element_type=F32)
            y[b, k * width : (k + 1) * width, :] = part.astype(BF16)
        return carry

    lax.fori_loop(0, blocks, body, 0)


def build_kernel(dims, handed, base, y, u, onsite, term, sent, stats, left, acc, *works):
    blocks, terms, width, _ = base.shape
    lanes = len(works)
    acc[...] = jnp.zeros_like(acc)

    def body(i, carry):
        for j in range(lanes):
            b = i * lanes + j
            work = works[j]
            block = handed[b]
            flipped = (block.astype(F32).T * (1.0 / width)).astype(BF16)
            carried = jnp.dot(
                base[b].reshape(terms * width, width), block, preferred_element_type=F32
            )
            work[...] = carried.astype(BF16)
            pieces = []
            for k in range(terms):
                added = jnp.dot(
                    flipped, work[k * width : (k + 1) * width, :], preferred_element_type=F32
                )
                piece = (base[b, k].astype(F32) + added).astype(BF16)
                left[b, k] = piece
                pieces.append(piece)
            total = jnp.dot(jnp.concatenate(pieces, axis=1), y[b], preferred_element_type=F32)
            value = jnp.where(live_of(dims[b], width), total, 0.0)
            term[b] = value
            sent[b] = value.astype(BF16)
            mine = u[b]
            acc[0] += folded(mine * mine)
            acc[1] += folded(mine * (onsite[b] * mine + value))
        return carry

    lax.fori_loop(0, blocks // lanes, body, 0)
    stats[...] = jnp.zeros_like(stats)
    for row in range(2):
        put_row(stats, row, acc[row])


def next_kernel(n_parts, entries, share, first, last, *refs):
    src, dims, *rest = refs
    parts, rest = rest[:n_parts], rest[n_parts:]
    (u, term, onsite, left, right, u_even, u_odd, t_even, t_odd, w_even, w_odd, *rest) = rest
    if last:
        un, tn, stats, x, acc, *lxs = rest
    else:
        un, tn, sent, stats, un_even, un_odd, x, acc, *lxs = rest
    blocks, width = u.shape[0], u.shape[1]
    terms = left.shape[1]
    sums = totals(parts)
    quotient = sums[1] / sums[0]
    eps = EPS if first else sums[5]
    scale = 1.0 / jnp.sqrt(sums[0] / entries + eps)
    grow = (1.0 + quotient) * scale

    def others(w, before, t, after, at):
        def body(b, carry):
            value = w[b].astype(F32) * (
                grow * before[b].astype(F32) - scale * t[b].astype(F32)
            )
            if not last:
                after[b] = value
            x[at + b] = value.astype(BF16)
            return carry

        lax.fori_loop(0, blocks, body, 0)

    others(w_even, u_even, t_even, None if last else un_even, 0)
    others(w_odd, u_odd, t_odd, None if last else un_odd, 2 * blocks)

    def own(b, carry):
        value = (grow * u[b] - scale * term[b]) / (onsite[b] + 1.0)
        un[b] = value
        x[blocks + b] = value.astype(BF16)
        return carry

    lax.fori_loop(0, blocks, own, 0)
    acc[...] = jnp.zeros_like(acc)

    def emit(b, value):
        tn[b] = value
        mine = un[b]
        acc[0] += folded(mine * mine)
        acc[1] += folded(mine * (onsite[b] * mine + value))
        if last:
            weight = 1.0 / (onsite[b] + 1.0)
            along = weight * mine
            guess = (1.0 + quotient) * along - weight * value
            acc[2] += folded(guess * guess)
            acc[3] += folded(guess * along)
            acc[4] += folded(along * along)
        else:
            sent[b] = value.astype(BF16)

    apply_terms(src, dims, x, left, right, lxs, blocks, terms, width, emit)
    stats[...] = jnp.zeros_like(stats)
    for row in range(5 if last else 2):
        put_row(stats, row, acc[row])
    lanes = stats.shape[1]
    if last:
        stats[5:6, :] = scalar_row(quotient * share, lanes)
    else:
        stats[5:6, :] = scalar_row((EPS * scale * scale if first else EPS) * share, lanes)


def final_kernel(n_parts, entries, *refs):
    parts, rest = refs[:n_parts], refs[n_parts:]
    u, term, onsite, *outs = rest
    sums = totals(parts)
    quotient = sums[1] / sums[0]
    scale = 1.0 / jnp.sqrt(sums[0] / entries + EPS)
    delta = quotient - sums[5]
    length = sums[2] + 2.0 * delta * sums[3] + delta * delta * sums[4]
    scale = scale / jnp.sqrt(length * scale * scale / entries + EPS)
    grow = (1.0 + quotient) * scale

    def body(b, carry):
        value = (grow * u[b] - scale * term[b]) / (onsite[b] + 1.0)
        outs[0][b] = value
        if len(outs) > 1:
            outs[1][b] = value.astype(BF16)
        return carry

    lax.fori_loop(0, u.shape[0], body, 0)


VMEM = pl.BlockSpec(memory_space=pltpu.VMEM)
SMEM = pl.BlockSpec(memory_space=pltpu.SMEM)
HBM = pl.BlockSpec(memory_space=pltpu.HBM)


def call(kernel, scalars, arrays, outs, scratch, far=()):
    return pl.pallas_call(
        kernel,
        out_shape=outs,
        in_specs=[SMEM] * len(scalars) + [VMEM] * len(arrays) + [HBM] * len(far),
        out_specs=[VMEM] * len(outs),
        scratch_shapes=scratch,
        compiler_params=pltpu.CompilerParams(vmem_limit_bytes=16 << 20),
    )(*scalars, *arrays, *[pltpu.with_memory_space_constraint(a, pltpu.HBM) for a in far])


def like(shape, dtype):
    return jax.ShapeDtypeStruct(shape, dtype)


def both_updates(*args):
    (
        wave_first,
        wave_second,
        onsite_first,
        onsite_second,
        left_first,
        right_first,
        left_base,
        right_second,
        sources,
        block_dims,
    ) = [a[0] if a.ndim > 3 else a for a in args]
    block_dims = pltpu.with_memory_space_constraint(block_dims, pltpu.HBM)
    blocks, width = wave_first.shape[0], wave_first.shape[1]
    terms = left_first.shape[1]
    count = lax.axis_size("sec")
    entries = float(blocks * count * width * width)

    lanes = max(j for j in (1, 2, 4) if blocks % j == 0)
    vec = (blocks, width, width)
    lxs = [pltpu.VMEM((width, terms * width), BF16)] * lanes
    x_shape = pltpu.VMEM((3 * blocks, width, width), BF16)
    acc_shape = pltpu.VMEM((5, 8, width), F32)
    stats_shape = like((8, width), F32)

    def later_steps(u, term, sent, stats, onsite, left, right, u_halo, w_halo, bundle=None):
        for step in range(1, STEPS):
            last = step == STEPS - 1
            t_halo = swapped(sent)
            parts = gathered_parts(stats)
            if last and bundle is not None:
                arrived = swapped(bundle)
            outs = [like(vec, F32), like(vec, F32)]
            if last:
                outs += [stats_shape]
            else:
                outs += [like(vec, BF16), stats_shape, like(vec, F32), like(vec, F32)]
            res = call(
                functools.partial(
                    next_kernel, len(parts), entries, 1.0 / count, step == 1, last
                ),
                [src, block_dims],
                [*parts, u, term, onsite, left, right, *u_halo, *t_halo, *w_halo],
                outs,
                [x_shape, acc_shape, *lxs],
            )
            if last:
                u, term, stats = res
            else:
                u, term, sent, stats, *u_halo = res
        out = (u, term, gathered_parts(stats))
        return out if bundle is None else (*out, arrived)

    def final(u, term, parts, onsite, narrow):
        outs = [like(vec, F32)] + ([like(vec, BF16)] if narrow else [])
        return call(
            functools.partial(final_kernel, len(parts), entries),
            [],
            [*parts, u, term, onsite],
            outs,
            [],
        )

    u, packed = call(
        prepare_kernel,
        [block_dims],
        [],
        [like(vec, F32), like(vec, BF16)],
        [pltpu.SemaphoreType.DMA((blocks,))],
        [wave_first],
    )
    halo_first = swapped(packed)
    weight, bundle = call(
        send_kernel,
        [block_dims],
        [packed],
        [like(vec, BF16), like((2 * blocks, width, width), BF16)],
        [pltpu.VMEM(vec, F32)] * 3 + [pltpu.SemaphoreType.DMA((3,))],
        [onsite_first, onsite_second, wave_second],
    )
    w_first = swapped(weight)
    here = lax.axis_index("sec")
    local = sources - here * blocks + blocks
    group = local // blocks
    src = jnp.where(here % 2 == 0, (2 - group) * blocks + local % blocks, local)

    pairs = max(j for j in (1, 2) if blocks % j == 0)
    term, sent, stats = call(
        start_kernel,
        [src, block_dims],
        [*halo_first, u],
        [like(vec, F32), like(vec, BF16), stats_shape],
        [
            pltpu.VMEM(vec, F32),
            pltpu.VMEM(left_first.shape, BF16),
            pltpu.VMEM(right_first.shape, BF16),
            x_shape,
            acc_shape,
            pltpu.SemaphoreType.DMA((3, blocks // pairs)),
            *lxs[:pairs],
        ],
        [onsite_first, left_first, right_first],
    )
    onsite, left, right = onsite_first, left_first, right_first
    u, term, parts, second = later_steps(
        u, term, sent, stats, onsite, left, right, halo_first, w_first, bundle
    )
    result_first, handed = final(u, term, parts, onsite, True)
    segs = lax.axis_size("seg")
    handed = lax.ppermute(handed, "seg", [(s, s + 1) for s in range(segs - 1)])

    halo_second = [part[:blocks] for part in second]
    w_second = [part[blocks:] for part in second]
    u, y = call(
        ahead_kernel,
        [src, block_dims],
        [*halo_second, wave_second, right_second],
        [like(vec, F32), like((blocks, terms * width, width), BF16)],
        [x_shape],
    )
    term, sent, stats, left_second = call(
        build_kernel,
        [block_dims],
        [handed, left_base, y, u, onsite_second],
        [like(vec, F32), like(vec, BF16), stats_shape, like(left_base.shape, BF16)],
        [acc_shape] + [pltpu.VMEM((terms * width, width), BF16)] * pairs,
    )
    u, term, parts = later_steps(
        u, term, sent, stats, onsite_second, left_second, right_second, halo_second, w_second
    )
    (result_second,) = final(u, term, parts, onsite_second, False)
    return result_first[None], result_second[None]


def solution(mesh):
    vector = P("seg", "sec", None, None)
    matrices = P("seg", "sec", None, None, None)
    placed = (vector,) * 4 + (matrices,) * 4 + (P("sec", None), P("sec"))
    return jax.shard_map(
        both_updates,
        mesh=mesh,
        in_specs=placed,
        out_specs=(vector, vector),
        check_vma=False,
    )
```

```python
import functools

import jax
import jax.numpy as jnp
from jax import lax
from jax.experimental import pallas as pl
from jax.experimental.pallas import tpu as pltpu
from jax.sharding import PartitionSpec as P

STEPS = 3
EPS = 1e-6
F32 = jnp.float32
BF16 = jnp.bfloat16


def even_pairs(count):
    return [(i, i ^ 1) for i in range(count) if i ^ 1 < count]


def odd_pairs(count):
    pairs = [(i, i + 1 if i % 2 else i - 1) for i in range(1, count)]
    return [(i, j) for i, j in pairs if j < count]


def swapped(block):
    count = lax.axis_size("sec")
    odd = lax.ppermute(block, "sec", odd_pairs(count))
    even = lax.ppermute(block, "sec", even_pairs(count))
    return even, odd


def gathered_parts(partial):
    count = lax.axis_size("sec")
    if count & (count - 1) or count < 2:
        return [lax.psum(partial, "sec")]
    pair = partial + lax.ppermute(partial, "sec", even_pairs(count))
    parts = [pair]
    for m in range(1, count // 2):
        parts += [lax.ppermute(pair, "sec", [(i, i ^ (2 * m)) for i in range(count)])]
    return parts


def after(value, *others):
    return lax.optimization_barrier((value, *others))[0]


def live_of(dim, width):
    rows = lax.broadcasted_iota(jnp.int32, (width, width), 0)
    cols = lax.broadcasted_iota(jnp.int32, (width, width), 1)
    return (rows < dim) & (cols < dim)


def folded(value):
    rows, lanes = value.shape
    return jnp.sum(value.reshape(rows // 8, 8, lanes), axis=0)


def put_row(ref, row, value):
    ref[row : row + 1, :] = jnp.sum(value, axis=0, keepdims=True)


def scalar_row(value, lanes):
    lane = lax.broadcasted_iota(jnp.int32, (1, lanes), 1)
    return jnp.where(lane == 0, value, 0.0)


def totals(refs):
    total = refs[0][...]
    for ref in refs[1:]:
        total = total + ref[...]
    return [jnp.sum(total[r : r + 1, :], axis=1, keepdims=True) for r in range(8)]


def apply_terms(src, dims, x, left, right, lxs, blocks, terms, width, emit, ready=None):
    lanes = len(lxs)

    def body(i, carry):
        if ready is not None:
            ready(i)
        for j in range(lanes):
            b = i * lanes + j
            for k in range(terms):
                part = jnp.dot(left[b, k], x[src[b, k]], preferred_element_type=F32)
                lxs[j][:, k * width : (k + 1) * width] = part.astype(BF16)
            total = jnp.dot(
                lxs[j][...],
                right[b].reshape(terms * width, width),
                preferred_element_type=F32,
            )
            emit(b, jnp.where(live_of(dims[b], width), total, 0.0))
        return carry

    lax.fori_loop(0, blocks // lanes, body, 0)


def prepare_kernel(dims, wave, u, packed, sems):
    blocks, width, _ = u.shape
    copies = [pltpu.make_async_copy(wave.at[b], u.at[b], sems.at[b]) for b in range(blocks)]
    for copy in copies:
        copy.start()
    for b in range(blocks):
        copies[b].wait()
        value = jnp.where(live_of(dims[b], width), u[b], 0.0)
        u[b] = value
        packed[b] = value.astype(BF16)


def send_kernel(dims, packed, onsite_hbm, later_hbm, wave_hbm, *rest):
    weight, bundle, onsite, later, wave, sems = rest
    del packed
    pairs = ((onsite_hbm, onsite), (wave_hbm, wave), (later_hbm, later))
    copies = [pltpu.make_async_copy(s, t, sems.at[i]) for i, (s, t) in enumerate(pairs)]
    for copy in copies:
        copy.start()
    blocks, width, _ = wave.shape
    copies[0].wait()

    def first(b, carry):
        weight[b] = (1.0 / (onsite[b] + 1.0)).astype(BF16)
        return carry

    lax.fori_loop(0, blocks, first, 0)
    copies[1].wait()
    copies[2].wait()

    def second(b, carry):
        bundle[b] = jnp.where(live_of(dims[b], width), wave[b], 0.0).astype(BF16)
        bundle[blocks + b] = (1.0 / (later[b] + 1.0)).astype(BF16)
        return carry

    lax.fori_loop(0, blocks, second, 0)


def start_kernel(src, dims, even, odd, u, onsite_hbm, left_hbm, right_hbm, *rest):
    term, sent, stats, onsite, left, right, x, acc, sems, *lxs = rest
    blocks, terms, width, _ = left.shape
    lanes = len(lxs)

    def copies_of(group):
        part = pl.ds(group * lanes, lanes)
        pairs = ((left_hbm, left), (right_hbm, right), (onsite_hbm, onsite))
        return [
            pltpu.make_async_copy(s.at[part], t.at[part], sems.at[i, group])
            for i, (s, t) in enumerate(pairs)
        ]

    for group in range(blocks // lanes):
        for copy in copies_of(group):
            copy.start()
    x[:blocks] = even[...]
    x[2 * blocks :] = odd[...]

    def first(b, carry):
        x[blocks + b] = u[b].astype(BF16)
        return carry

    lax.fori_loop(0, blocks, first, 0)
    acc[...] = jnp.zeros_like(acc)

    def emit(b, value):
        term[b] = value
        sent[b] = value.astype(BF16)
        mine = u[b]
        acc[0] += folded(mine * mine)
        acc[1] += folded(mine * (onsite[b] * mine + value))

    def ready(group):
        for copy in copies_of(group):
            copy.wait()

    apply_terms(src, dims, x, left, right, lxs, blocks, terms, width, emit, ready)
    stats[...] = jnp.zeros_like(stats)
    for row in range(2):
        put_row(stats, row, acc[row])


def ahead_kernel(src, dims, even, odd, wave, right, u, y, x):
    blocks, terms, width, _ = right.shape
    x[:blocks] = even[...]
    x[2 * blocks :] = odd[...]

    def first(b, carry):
        value = jnp.where(live_of(dims[b], width), wave[b], 0.0)
        u[b] = value
        x[blocks + b] = value.astype(BF16)
        return carry

    lax.fori_loop(0, blocks, first, 0)

    def body(b, carry):
        for k in range(terms):
            part = jnp.dot(x[src[b, k]], right[b, k], preferred_element_type=F32)
            y[b, k * width : (k + 1) * width, :] = part.astype(BF16)
        return carry

    lax.fori_loop(0, blocks, body, 0)


def build_kernel(dims, handed, base, y, u, onsite, term, sent, stats, left, acc, *works):
    blocks, terms, width, _ = base.shape
    lanes = len(works)
    acc[...] = jnp.zeros_like(acc)

    def body(i, carry):
        for j in range(lanes):
            b = i * lanes + j
            work = works[j]
            block = handed[b]
            flipped = (block.astype(F32).T * (1.0 / width)).astype(BF16)
            carried = jnp.dot(
                base[b].reshape(terms * width, width), block, preferred_element_type=F32
            )
            work[...] = carried.astype(BF16)
            pieces = []
            for k in range(terms):
                added = jnp.dot(
                    flipped, work[k * width : (k + 1) * width, :], preferred_element_type=F32
                )
                piece = (base[b, k].astype(F32) + added).astype(BF16)
                left[b, k] = piece
                pieces.append(piece)
            total = jnp.dot(jnp.concatenate(pieces, axis=1), y[b], preferred_element_type=F32)
            value = jnp.where(live_of(dims[b], width), total, 0.0)
            term[b] = value
            sent[b] = value.astype(BF16)
            mine = u[b]
            acc[0] += folded(mine * mine)
            acc[1] += folded(mine * (onsite[b] * mine + value))
        return carry

    lax.fori_loop(0, blocks // lanes, body, 0)
    stats[...] = jnp.zeros_like(stats)
    for row in range(2):
        put_row(stats, row, acc[row])


def next_kernel(n_parts, entries, share, first, last, *refs):
    src, dims, *rest = refs
    parts, rest = rest[:n_parts], rest[n_parts:]
    (u, term, onsite, left, right, u_even, u_odd, t_even, t_odd, w_even, w_odd, *rest) = rest
    if last:
        un, tn, stats, x, acc, *lxs = rest
    else:
        un, tn, sent, stats, un_even, un_odd, x, acc, *lxs = rest
    blocks, width = u.shape[0], u.shape[1]
    terms = left.shape[1]
    sums = totals(parts)
    quotient = sums[1] / sums[0]
    eps = EPS if first else sums[5]
    scale = 1.0 / jnp.sqrt(sums[0] / entries + eps)
    grow = (1.0 + quotient) * scale

    def neighbour(b, w, before, t, kept_at, at):
        value = w[b].astype(F32) * (grow * before[b].astype(F32) - scale * t[b].astype(F32))
        if kept_at is not None:
            kept_at[b] = value
        x[at + b] = value.astype(BF16)

    def move(b, carry):
        neighbour(b, w_even, u_even, t_even, None if last else un_even, 0)
        neighbour(b, w_odd, u_odd, t_odd, None if last else un_odd, 2 * blocks)
        value = (grow * u[b] - scale * term[b]) / (onsite[b] + 1.0)
        un[b] = value
        x[blocks + b] = value.astype(BF16)
        return carry

    lax.fori_loop(0, blocks, move, 0, unroll=2 if blocks % 2 == 0 else 1)
    acc[...] = jnp.zeros_like(acc)

    def emit(b, value):
        tn[b] = value
        mine = un[b]
        acc[0] += folded(mine * mine)
        acc[1] += folded(mine * (onsite[b] * mine + value))
        if last:
            weight = 1.0 / (onsite[b] + 1.0)
            along = weight * mine
            guess = (1.0 + quotient) * along - weight * value
            acc[2] += folded(guess * guess)
            acc[3] += folded(guess * along)
            acc[4] += folded(along * along)
        else:
            sent[b] = value.astype(BF16)

    apply_terms(src, dims, x, left, right, lxs, blocks, terms, width, emit)
    stats[...] = jnp.zeros_like(stats)
    for row in range(5 if last else 2):
        put_row(stats, row, acc[row])
    lanes = stats.shape[1]
    if last:
        stats[5:6, :] = scalar_row(quotient * share, lanes)
    else:
        stats[5:6, :] = scalar_row((EPS * scale * scale if first else EPS) * share, lanes)


def final_kernel(n_parts, entries, *refs):
    parts, rest = refs[:n_parts], refs[n_parts:]
    u, term, onsite, out, *held = rest
    sums = totals(parts)
    quotient = sums[1] / sums[0]
    scale = 1.0 / jnp.sqrt(sums[0] / entries + EPS)
    delta = quotient - sums[5]
    length = sums[2] + 2.0 * delta * sums[3] + delta * delta * sums[4]
    scale = scale / jnp.sqrt(length * scale * scale / entries + EPS)
    grow = (1.0 + quotient) * scale
    blocks = u.shape[0]
    lanes = 2 if blocks % 2 == 0 else 1

    def copy_of(i):
        part = pl.ds(i * lanes, lanes)
        return pltpu.make_async_copy(held[0].at[part], out.at[part], held[1].at[i])

    for i in range(blocks // lanes):
        for b in range(i * lanes, (i + 1) * lanes):
            value = (grow * u[b] - scale * term[b]) / (onsite[b] + 1.0)
            if held:
                held[0][b] = value
            else:
                out[b] = value.astype(out.dtype)
        if held:
            copy_of(i).start()
    if held:
        for i in range(blocks // lanes):
            copy_of(i).wait()


VMEM = pl.BlockSpec(memory_space=pltpu.VMEM)
SMEM = pl.BlockSpec(memory_space=pltpu.SMEM)
HBM = pl.BlockSpec(memory_space=pltpu.HBM)


def call(kernel, scalars, arrays, outs, scratch, far=(), out_spec=None):
    return pl.pallas_call(
        kernel,
        out_shape=outs,
        in_specs=[SMEM] * len(scalars) + [VMEM] * len(arrays) + [HBM] * len(far),
        out_specs=[out_spec or VMEM] * len(outs),
        scratch_shapes=scratch,
        compiler_params=pltpu.CompilerParams(vmem_limit_bytes=16 << 20),
    )(*scalars, *arrays, *[pltpu.with_memory_space_constraint(a, pltpu.HBM) for a in far])


def like(shape, dtype):
    return jax.ShapeDtypeStruct(shape, dtype)


def both_updates(*args):
    (
        wave_first,
        wave_second,
        onsite_first,
        onsite_second,
        left_first,
        right_first,
        left_base,
        right_second,
        sources,
        block_dims,
    ) = [a[0] if a.ndim > 3 else a for a in args]
    block_dims = pltpu.with_memory_space_constraint(block_dims, pltpu.HBM)
    blocks, width = wave_first.shape[0], wave_first.shape[1]
    terms = left_first.shape[1]
    count = lax.axis_size("sec")
    entries = float(blocks * count * width * width)

    lanes = max(j for j in (1, 2, 4) if blocks % j == 0)
    vec = (blocks, width, width)
    lxs = [pltpu.VMEM((width, terms * width), BF16)] * lanes
    x_shape = pltpu.VMEM((3 * blocks, width, width), BF16)
    acc_shape = pltpu.VMEM((5, 8, width), F32)
    stats_shape = like((8, width), F32)

    def later_steps(u, term, sent, stats, onsite, left, right, u_halo, w_halo, bundle=None):
        for step in range(1, STEPS):
            last = step == STEPS - 1
            t_halo = swapped(sent)
            parts = gathered_parts(stats)
            if last and bundle is not None:
                arrived = swapped(bundle)
            outs = [like(vec, F32), like(vec, F32)]
            if last:
                outs += [stats_shape]
            else:
                outs += [like(vec, BF16), stats_shape, like(vec, F32), like(vec, F32)]
            res = call(
                functools.partial(
                    next_kernel, len(parts), entries, 1.0 / count, step == 1, last
                ),
                [src, block_dims],
                [*parts, u, term, onsite, left, right, *u_halo, *t_halo, *w_halo],
                outs,
                [x_shape, acc_shape, *lxs],
            )
            if last:
                u, term, stats = res
            else:
                u, term, sent, stats, *u_halo = res
        out = (u, term, gathered_parts(stats))
        return out if bundle is None else (*out, arrived)

    def final(u, term, parts, onsite, narrow):
        held = [] if narrow else [pltpu.VMEM(vec, F32), pltpu.SemaphoreType.DMA((blocks,))]
        (out,) = call(
            functools.partial(final_kernel, len(parts), entries),
            [],
            [*parts, u, term, onsite],
            [like(vec, BF16 if narrow else F32)],
            held,
            (),
            VMEM if narrow else HBM,
        )
        return out

    u, packed = call(
        prepare_kernel,
        [block_dims],
        [],
        [like(vec, F32), like(vec, BF16)],
        [pltpu.SemaphoreType.DMA((blocks,))],
        [wave_first],
    )
    halo_first = swapped(packed)
    weight, bundle = call(
        send_kernel,
        [block_dims],
        [packed],
        [like(vec, BF16), like((2 * blocks, width, width), BF16)],
        [pltpu.VMEM(vec, F32)] * 3 + [pltpu.SemaphoreType.DMA((3,))],
        [onsite_first, onsite_second, wave_second],
    )
    w_first = swapped(weight)
    here = lax.axis_index("sec")
    local = sources - here * blocks + blocks
    group = local // blocks
    src = jnp.where(here % 2 == 0, (2 - group) * blocks + local % blocks, local)

    pairs = max(j for j in (1, 2) if blocks % j == 0)
    term, sent, stats = call(
        start_kernel,
        [src, block_dims],
        [*halo_first, u],
        [like(vec, F32), like(vec, BF16), stats_shape],
        [
            pltpu.VMEM(vec, F32),
            pltpu.VMEM(left_first.shape, BF16),
            pltpu.VMEM(right_first.shape, BF16),
            x_shape,
            acc_shape,
            pltpu.SemaphoreType.DMA((3, blocks // pairs)),
            *lxs[:pairs],
        ],
        [onsite_first, left_first, right_first],
    )
    onsite, left, right = onsite_first, left_first, right_first
    u, term, parts, second = later_steps(
        u, term, sent, stats, onsite, left, right, halo_first, w_first, bundle
    )
    handed = final(u, term, parts, onsite, True)
    ended = (u, term, parts, onsite)
    segs = lax.axis_size("seg")
    handed = lax.ppermute(handed, "seg", [(s, s + 1) for s in range(segs - 1)])

    halo_second = [part[:blocks] for part in second]
    w_second = [part[blocks:] for part in second]
    u, y = call(
        ahead_kernel,
        [src, block_dims],
        [*halo_second, wave_second, right_second],
        [like(vec, F32), like((blocks, terms * width, width), BF16)],
        [x_shape],
    )
    term, sent, stats, left_second = call(
        build_kernel,
        [block_dims],
        [handed, left_base, y, u, onsite_second],
        [like(vec, F32), like(vec, BF16), stats_shape, like(left_base.shape, BF16)],
        [acc_shape] + [pltpu.VMEM((terms * width, width), BF16)] * lanes,
    )
    u_first, term_first, parts_first, onsite = ended
    result_first = final(after(u_first, stats), term_first, parts_first, onsite, False)
    u, term, parts = later_steps(
        u, term, sent, stats, onsite_second, left_second, right_second, halo_second, w_second
    )
    result_second = final(u, term, parts, onsite_second, False)
    return result_first[None], result_second[None]


def solution(mesh):
    vector = P("seg", "sec", None, None)
    matrices = P("seg", "sec", None, None, None)
    placed = (vector,) * 4 + (matrices,) * 4 + (P("sec", None), P("sec"))
    return jax.shard_map(
        both_updates,
        mesh=mesh,
        in_specs=placed,
        out_specs=(vector, vector),
        check_vma=False,
    )
```

```python
import functools

import jax
import jax.numpy as jnp
from jax import lax
from jax.experimental import pallas as pl
from jax.experimental.pallas import tpu as pltpu
from jax.sharding import PartitionSpec as P

STEPS = 3
EPS = 1e-6
F32 = jnp.float32
BF16 = jnp.bfloat16


def even_pairs(count):
    return [(i, i ^ 1) for i in range(count) if i ^ 1 < count]


def odd_pairs(count):
    pairs = [(i, i + 1 if i % 2 else i - 1) for i in range(1, count)]
    return [(i, j) for i, j in pairs if j < count]


def swapped(block):
    count = lax.axis_size("sec")
    odd = lax.ppermute(block, "sec", odd_pairs(count))
    even = lax.ppermute(block, "sec", even_pairs(count))
    return even, odd


def gathered_parts(partial):
    count = lax.axis_size("sec")
    if count & (count - 1) or count < 2:
        return [lax.psum(partial, "sec")]
    pair = partial + lax.ppermute(partial, "sec", even_pairs(count))
    parts = [pair]
    for m in range(1, count // 2):
        parts += [lax.ppermute(pair, "sec", [(i, i ^ (2 * m)) for i in range(count)])]
    return parts


def after(value, *others):
    return lax.optimization_barrier((value, *others))[0]


def live_of(dim, width):
    rows = lax.broadcasted_iota(jnp.int32, (width, width), 0)
    cols = lax.broadcasted_iota(jnp.int32, (width, width), 1)
    return (rows < dim) & (cols < dim)


def folded(value):
    rows, lanes = value.shape
    return jnp.sum(value.reshape(rows // 8, 8, lanes), axis=0)


def put_row(ref, row, value):
    ref[row : row + 1, :] = jnp.sum(value, axis=0, keepdims=True)


def scalar_row(value, lanes):
    lane = lax.broadcasted_iota(jnp.int32, (1, lanes), 1)
    return jnp.where(lane == 0, value, 0.0)


def totals(refs):
    total = refs[0][...]
    for ref in refs[1:]:
        total = total + ref[...]
    return [jnp.sum(total[r : r + 1, :], axis=1, keepdims=True) for r in range(8)]


def apply_terms(src, dims, x, left, right, lxs, blocks, terms, width, emit, ready=None):
    lanes = len(lxs)

    def body(i, carry):
        if ready is not None:
            ready(i)
        for j in range(lanes):
            b = i * lanes + j
            for k in range(terms):
                part = jnp.dot(left[b, k], x[src[b, k]], preferred_element_type=F32)
                lxs[j][:, k * width : (k + 1) * width] = part.astype(BF16)
            total = jnp.dot(
                lxs[j][...],
                right[b].reshape(terms * width, width),
                preferred_element_type=F32,
            )
            emit(b, jnp.where(live_of(dims[b], width), total, 0.0))
        return carry

    lax.fori_loop(0, blocks // lanes, body, 0)


def prepare_kernel(ready, dims, wave, u, packed, sems):
    blocks, width, _ = u.shape
    copies = [pltpu.make_async_copy(wave.at[b], u.at[b], sems.at[b]) for b in range(blocks)]
    for copy in copies:
        copy.start()
    ready()
    for b in range(blocks):
        copies[b].wait()
        value = jnp.where(live_of(dims[b], width), u[b], 0.0)
        u[b] = value
        packed[b] = value.astype(BF16)


def send_kernel(ready, dims, packed, onsite_hbm, later_hbm, wave_hbm, *rest):
    weight, bundle, onsite, later, wave, sems = rest
    del packed
    pairs = ((onsite_hbm, onsite), (wave_hbm, wave), (later_hbm, later))
    copies = [pltpu.make_async_copy(s, t, sems.at[i]) for i, (s, t) in enumerate(pairs)]
    for copy in copies:
        copy.start()
    blocks, width, _ = wave.shape
    copies[0].wait()

    def first(b, carry):
        weight[b] = (1.0 / (onsite[b] + 1.0)).astype(BF16)
        return carry

    lax.fori_loop(0, blocks, first, 0)
    ready()
    copies[1].wait()
    copies[2].wait()

    def second(b, carry):
        bundle[b] = jnp.where(live_of(dims[b], width), wave[b], 0.0).astype(BF16)
        bundle[blocks + b] = (1.0 / (later[b] + 1.0)).astype(BF16)
        return carry

    lax.fori_loop(0, blocks, second, 0)


def start_kernel(scalars, src, dims, even, odd, u, onsite_hbm, left_hbm, right_hbm, *rest):
    term, sent, stats, onsite, left, right, x, acc, sems, *lxs = rest
    blocks, terms, width, _ = left.shape
    lanes = len(lxs)

    def copies_of(group):
        part = pl.ds(group * lanes, lanes)
        pairs = ((left_hbm, left), (right_hbm, right), (onsite_hbm, onsite))
        return [
            pltpu.make_async_copy(s.at[part], t.at[part], sems.at[i, group])
            for i, (s, t) in enumerate(pairs)
        ]

    for group in range(blocks // lanes):
        for copy in copies_of(group):
            copy.start()
    x[:blocks] = even[...]
    x[2 * blocks :] = odd[...]

    def first(b, carry):
        x[blocks + b] = u[b].astype(BF16)
        return carry

    lax.fori_loop(0, blocks, first, 0)
    acc[...] = jnp.zeros_like(acc)

    def emit(b, value):
        term[b] = value
        sent[b] = value.astype(BF16)
        mine = u[b]
        acc[0] += folded(mine * mine)
        acc[1] += folded(mine * (onsite[b] * mine + value))

    def ready(group):
        for copy in copies_of(group):
            copy.wait()

    scalars()
    apply_terms(src, dims, x, left, right, lxs, blocks, terms, width, emit, ready)
    stats[...] = jnp.zeros_like(stats)
    for row in range(2):
        put_row(stats, row, acc[row])


def ahead_kernel(ready, src, dims, even, odd, wave, right, u, y, x):
    blocks, terms, width, _ = right.shape
    x[:blocks] = even[...]
    x[2 * blocks :] = odd[...]
    ready()

    def first(b, carry):
        value = jnp.where(live_of(dims[b], width), wave[b], 0.0)
        u[b] = value
        x[blocks + b] = value.astype(BF16)
        return carry

    lax.fori_loop(0, blocks, first, 0)

    def body(b, carry):
        for k in range(terms):
            part = jnp.dot(x[src[b, k]], right[b, k], preferred_element_type=F32)
            y[b, k * width : (k + 1) * width, :] = part.astype(BF16)
        return carry

    lax.fori_loop(0, blocks, body, 0)


def build_kernel(ready, dims, handed, base, y, u, onsite, term, sent, stats, left, acc, *works):
    blocks, terms, width, _ = base.shape
    lanes = len(works)
    acc[...] = jnp.zeros_like(acc)
    ready()

    def body(i, carry):
        for j in range(lanes):
            b = i * lanes + j
            work = works[j]
            block = handed[b]
            flipped = (block.astype(F32).T * (1.0 / width)).astype(BF16)
            carried = jnp.dot(
                base[b].reshape(terms * width, width), block, preferred_element_type=F32
            )
            work[...] = carried.astype(BF16)
            pieces = []
            for k in range(terms):
                added = jnp.dot(
                    flipped, work[k * width : (k + 1) * width, :], preferred_element_type=F32
                )
                piece = (base[b, k].astype(F32) + added).astype(BF16)
                left[b, k] = piece
                pieces.append(piece)
            total = jnp.dot(jnp.concatenate(pieces, axis=1), y[b], preferred_element_type=F32)
            value = jnp.where(live_of(dims[b], width), total, 0.0)
            term[b] = value
            sent[b] = value.astype(BF16)
            mine = u[b]
            acc[0] += folded(mine * mine)
            acc[1] += folded(mine * (onsite[b] * mine + value))
        return carry

    lax.fori_loop(0, blocks // lanes, body, 0)
    stats[...] = jnp.zeros_like(stats)
    for row in range(2):
        put_row(stats, row, acc[row])


def next_kernel(n_parts, entries, share, first, last, scalars, *refs):
    src, dims, *rest = refs
    parts, rest = rest[:n_parts], rest[n_parts:]
    (u, term, onsite, left, right, u_even, u_odd, t_even, t_odd, w_even, w_odd, *rest) = rest
    if last:
        un, tn, stats, x, acc, *lxs = rest
    else:
        un, tn, sent, stats, un_even, un_odd, x, acc, *lxs = rest
    blocks, width = u.shape[0], u.shape[1]
    terms = left.shape[1]
    sums = totals(parts)
    quotient = sums[1] / sums[0]
    eps = EPS if first else sums[5]
    scale = 1.0 / jnp.sqrt(sums[0] / entries + eps)
    grow = (1.0 + quotient) * scale

    def neighbour(b, w, before, t, kept_at, at):
        value = w[b].astype(F32) * (grow * before[b].astype(F32) - scale * t[b].astype(F32))
        if kept_at is not None:
            kept_at[b] = value
        x[at + b] = value.astype(BF16)

    def move(b, carry):
        neighbour(b, w_even, u_even, t_even, None if last else un_even, 0)
        neighbour(b, w_odd, u_odd, t_odd, None if last else un_odd, 2 * blocks)
        value = (grow * u[b] - scale * term[b]) / (onsite[b] + 1.0)
        un[b] = value
        x[blocks + b] = value.astype(BF16)
        return carry

    lax.fori_loop(0, blocks, move, 0, unroll=2 if blocks % 2 == 0 else 1)
    acc[...] = jnp.zeros_like(acc)

    def emit(b, value):
        tn[b] = value
        mine = un[b]
        acc[0] += folded(mine * mine)
        acc[1] += folded(mine * (onsite[b] * mine + value))
        if last:
            weight = 1.0 / (onsite[b] + 1.0)
            along = weight * mine
            guess = (1.0 + quotient) * along - weight * value
            acc[2] += folded(guess * guess)
            acc[3] += folded(guess * along)
            acc[4] += folded(along * along)
        else:
            sent[b] = value.astype(BF16)

    scalars()
    apply_terms(src, dims, x, left, right, lxs, blocks, terms, width, emit)
    stats[...] = jnp.zeros_like(stats)
    for row in range(5 if last else 2):
        put_row(stats, row, acc[row])
    lanes = stats.shape[1]
    if last:
        stats[5:6, :] = scalar_row(quotient * share, lanes)
    else:
        stats[5:6, :] = scalar_row((EPS * scale * scale if first else EPS) * share, lanes)


def final_kernel(n_parts, entries, *refs):
    parts, rest = refs[:n_parts], refs[n_parts:]
    u, term, onsite, out, *held = rest
    sums = totals(parts)
    quotient = sums[1] / sums[0]
    scale = 1.0 / jnp.sqrt(sums[0] / entries + EPS)
    delta = quotient - sums[5]
    length = sums[2] + 2.0 * delta * sums[3] + delta * delta * sums[4]
    scale = scale / jnp.sqrt(length * scale * scale / entries + EPS)
    grow = (1.0 + quotient) * scale
    blocks = u.shape[0]
    lanes = 2 if blocks % 2 == 0 else 1

    def copy_of(i):
        part = pl.ds(i * lanes, lanes)
        return pltpu.make_async_copy(held[0].at[part], out.at[part], held[1].at[i])

    for i in range(blocks // lanes):
        for b in range(i * lanes, (i + 1) * lanes):
            value = (grow * u[b] - scale * term[b]) / (onsite[b] + 1.0)
            if held:
                held[0][b] = value
            else:
                out[b] = value.astype(out.dtype)
        if held:
            copy_of(i).start()
    if held:
        for i in range(blocks // lanes):
            copy_of(i).wait()


VMEM = pl.BlockSpec(memory_space=pltpu.VMEM)
HBM = pl.BlockSpec(memory_space=pltpu.HBM)


def call(kernel, scalars, arrays, outs, scratch, far=(), out_spec=None):
    count = len(scalars)

    def body(*refs):
        tables, sems = refs[-1 - count : -1], refs[-1]
        copies = [pltpu.make_async_copy(refs[i], tables[i], sems.at[i]) for i in range(count)]
        for copy in copies:
            copy.start()

        def ready():
            for copy in copies:
                copy.wait()

        kernel(ready, *tables, *refs[count : -1 - count])

    held = [pltpu.SMEM(a.shape, a.dtype) for a in scalars]
    held += [pltpu.SemaphoreType.DMA((count,))] if count else []
    return pl.pallas_call(
        body if count else kernel,
        out_shape=outs,
        in_specs=[HBM] * count + [VMEM] * len(arrays) + [HBM] * len(far),
        out_specs=[out_spec or VMEM] * len(outs),
        scratch_shapes=[*scratch, *held],
        compiler_params=pltpu.CompilerParams(vmem_limit_bytes=16 << 20),
    )(
        *[pltpu.with_memory_space_constraint(a, pltpu.HBM) for a in scalars],
        *arrays,
        *[pltpu.with_memory_space_constraint(a, pltpu.HBM) for a in far],
    )


def like(shape, dtype):
    return jax.ShapeDtypeStruct(shape, dtype)


def both_updates(*args):
    (
        wave_first,
        wave_second,
        onsite_first,
        onsite_second,
        left_first,
        right_first,
        left_base,
        right_second,
        sources,
        block_dims,
    ) = [a[0] if a.ndim > 3 else a for a in args]
    blocks, width = wave_first.shape[0], wave_first.shape[1]
    terms = left_first.shape[1]
    count = lax.axis_size("sec")
    entries = float(blocks * count * width * width)

    lanes = max(j for j in (1, 2, 4) if blocks % j == 0)
    vec = (blocks, width, width)
    lxs = [pltpu.VMEM((width, terms * width), BF16)] * lanes
    x_shape = pltpu.VMEM((3 * blocks, width, width), BF16)
    acc_shape = pltpu.VMEM((5, 8, width), F32)
    stats_shape = like((8, width), F32)

    def later_steps(u, term, sent, stats, onsite, left, right, u_halo, w_halo, bundle=None):
        for step in range(1, STEPS):
            last = step == STEPS - 1
            t_halo = swapped(sent)
            parts = gathered_parts(stats)
            if last and bundle is not None:
                arrived = swapped(bundle)
            outs = [like(vec, F32), like(vec, F32)]
            if last:
                outs += [stats_shape]
            else:
                outs += [like(vec, BF16), stats_shape, like(vec, F32), like(vec, F32)]
            res = call(
                functools.partial(
                    next_kernel, len(parts), entries, 1.0 / count, step == 1, last
                ),
                [src, block_dims],
                [*parts, u, term, onsite, left, right, *u_halo, *t_halo, *w_halo],
                outs,
                [x_shape, acc_shape, *lxs],
            )
            if last:
                u, term, stats = res
            else:
                u, term, sent, stats, *u_halo = res
        out = (u, term, gathered_parts(stats))
        return out if bundle is None else (*out, arrived)

    def final(u, term, parts, onsite, narrow):
        held = [] if narrow else [pltpu.VMEM(vec, F32), pltpu.SemaphoreType.DMA((blocks,))]
        (out,) = call(
            functools.partial(final_kernel, len(parts), entries),
            [],
            [*parts, u, term, onsite],
            [like(vec, BF16 if narrow else F32)],
            held,
            (),
            VMEM if narrow else HBM,
        )
        return out

    u, packed = call(
        prepare_kernel,
        [block_dims],
        [],
        [like(vec, F32), like(vec, BF16)],
        [pltpu.SemaphoreType.DMA((blocks,))],
        [wave_first],
    )
    halo_first = swapped(packed)
    weight, bundle = call(
        send_kernel,
        [block_dims],
        [packed],
        [like(vec, BF16), like((2 * blocks, width, width), BF16)],
        [pltpu.VMEM(vec, F32)] * 3 + [pltpu.SemaphoreType.DMA((3,))],
        [onsite_first, onsite_second, wave_second],
    )
    w_first = swapped(weight)
    here = lax.axis_index("sec")
    local = sources - here * blocks + blocks
    group = local // blocks
    src = jnp.where(here % 2 == 0, (2 - group) * blocks + local % blocks, local)

    pairs = max(j for j in (1, 2) if blocks % j == 0)
    term, sent, stats = call(
        start_kernel,
        [src, block_dims],
        [*halo_first, u],
        [like(vec, F32), like(vec, BF16), stats_shape],
        [
            pltpu.VMEM(vec, F32),
            pltpu.VMEM(left_first.shape, BF16),
            pltpu.VMEM(right_first.shape, BF16),
            x_shape,
            acc_shape,
            pltpu.SemaphoreType.DMA((3, blocks // pairs)),
            *lxs[:pairs],
        ],
        [onsite_first, left_first, right_first],
    )
    onsite, left, right = onsite_first, left_first, right_first
    u, term, parts, second = later_steps(
        u, term, sent, stats, onsite, left, right, halo_first, w_first, bundle
    )
    handed = final(u, term, parts, onsite, True)
    ended = (u, term, parts, onsite)
    segs = lax.axis_size("seg")
    handed = lax.ppermute(handed, "seg", [(s, s + 1) for s in range(segs - 1)])

    halo_second = [part[:blocks] for part in second]
    w_second = [part[blocks:] for part in second]
    u, y = call(
        ahead_kernel,
        [src, block_dims],
        [*halo_second, wave_second, right_second],
        [like(vec, F32), like((blocks, terms * width, width), BF16)],
        [x_shape],
    )
    term, sent, stats, left_second = call(
        build_kernel,
        [block_dims],
        [handed, left_base, y, u, onsite_second],
        [like(vec, F32), like(vec, BF16), stats_shape, like(left_base.shape, BF16)],
        [acc_shape] + [pltpu.VMEM((terms * width, width), BF16)] * lanes,
    )
    u_first, term_first, parts_first, onsite = ended
    result_first = final(after(u_first, stats), term_first, parts_first, onsite, False)
    u, term, parts = later_steps(
        u, term, sent, stats, onsite_second, left_second, right_second, halo_second, w_second
    )
    result_second = final(u, term, parts, onsite_second, False)
    return result_first[None], result_second[None]


def solution(mesh):
    vector = P("seg", "sec", None, None)
    matrices = P("seg", "sec", None, None, None)
    placed = (vector,) * 4 + (matrices,) * 4 + (P("sec", None), P("sec"))
    return jax.shard_map(
        both_updates,
        mesh=mesh,
        in_specs=placed,
        out_specs=(vector, vector),
        check_vma=False,
    )
```

```python
import functools

import jax
import jax.numpy as jnp
from jax import lax
from jax.experimental import pallas as pl
from jax.experimental.pallas import tpu as pltpu
from jax.sharding import PartitionSpec as P

STEPS = 3
EPS = 1e-6
F32 = jnp.float32
BF16 = jnp.bfloat16


def even_pairs(count):
    return [(i, i ^ 1) for i in range(count) if i ^ 1 < count]


def odd_pairs(count):
    pairs = [(i, i + 1 if i % 2 else i - 1) for i in range(1, count)]
    return [(i, j) for i, j in pairs if j < count]


def swapped(block):
    count = lax.axis_size("sec")
    odd = lax.ppermute(block, "sec", odd_pairs(count))
    even = lax.ppermute(block, "sec", even_pairs(count))
    return even, odd


def gathered_parts(partial):
    count = lax.axis_size("sec")
    if count & (count - 1) or count < 2:
        return [lax.psum(partial, "sec")]
    pair = partial + lax.ppermute(partial, "sec", even_pairs(count))
    parts = [pair]
    for m in range(1, count // 2):
        parts += [lax.ppermute(pair, "sec", [(i, i ^ (2 * m)) for i in range(count)])]
    return parts


def after(value, *others):
    return lax.optimization_barrier((value, *others))[0]


def live_of(dim, width):
    rows = lax.broadcasted_iota(jnp.int32, (width, width), 0)
    cols = lax.broadcasted_iota(jnp.int32, (width, width), 1)
    return (rows < dim) & (cols < dim)


def folded(value):
    rows, lanes = value.shape
    return jnp.sum(value.reshape(rows // 8, 8, lanes), axis=0)


def put_row(ref, row, value):
    ref[row : row + 1, :] = jnp.sum(value, axis=0, keepdims=True)


def scalar_row(value, lanes):
    lane = lax.broadcasted_iota(jnp.int32, (1, lanes), 1)
    return jnp.where(lane == 0, value, 0.0)


def totals(refs):
    total = refs[0][...]
    for ref in refs[1:]:
        total = total + ref[...]
    return [jnp.sum(total[r : r + 1, :], axis=1, keepdims=True) for r in range(8)]


def apply_terms(src, dims, x, left, right, lxs, blocks, terms, width, emit, ready=None):
    lanes = len(lxs)

    def body(i, carry):
        if ready is not None:
            ready(i)
        for j in range(lanes):
            b = i * lanes + j
            for k in range(terms):
                part = jnp.dot(left[b, k], x[src[b, k]], preferred_element_type=F32)
                lxs[j][:, k * width : (k + 1) * width] = part.astype(BF16)
            total = jnp.dot(
                lxs[j][...],
                right[b].reshape(terms * width, width),
                preferred_element_type=F32,
            )
            emit(b, jnp.where(live_of(dims[b], width), total, 0.0))
        return carry

    lax.fori_loop(0, blocks // lanes, body, 0)


def prepare_kernel(ready, dims, wave, u, packed, sems):
    blocks, width, _ = u.shape
    copies = [pltpu.make_async_copy(wave.at[b], u.at[b], sems.at[b]) for b in range(blocks)]
    for copy in copies:
        copy.start()
    ready()
    for b in range(blocks):
        copies[b].wait()
        value = jnp.where(live_of(dims[b], width), u[b], 0.0)
        u[b] = value
        packed[b] = value.astype(BF16)


def send_kernel(ready, dims, packed, onsite_hbm, later_hbm, wave_hbm, *rest):
    weight, bundle, onsite, later, wave, sems = rest
    del packed
    pairs = ((onsite_hbm, onsite), (wave_hbm, wave), (later_hbm, later))
    copies = [pltpu.make_async_copy(s, t, sems.at[i]) for i, (s, t) in enumerate(pairs)]
    for copy in copies:
        copy.start()
    blocks, width, _ = wave.shape
    copies[0].wait()

    def first(b, carry):
        weight[b] = (1.0 / (onsite[b] + 1.0)).astype(BF16)
        return carry

    lax.fori_loop(0, blocks, first, 0)
    ready()
    copies[1].wait()
    copies[2].wait()

    def second(b, carry):
        bundle[b] = jnp.where(live_of(dims[b], width), wave[b], 0.0).astype(BF16)
        bundle[blocks + b] = (1.0 / (later[b] + 1.0)).astype(BF16)
        return carry

    lax.fori_loop(0, blocks, second, 0)


def start_kernel(scalars, src, dims, even, odd, u, onsite_hbm, left_hbm, right_hbm, *rest):
    term, sent, stats, onsite, left, right, x, acc, sems, *lxs = rest
    blocks, terms, width, _ = left.shape
    lanes = len(lxs)

    def copies_of(group):
        part = pl.ds(group * lanes, lanes)
        pairs = ((left_hbm, left), (right_hbm, right), (onsite_hbm, onsite))
        return [
            pltpu.make_async_copy(s.at[part], t.at[part], sems.at[i, group])
            for i, (s, t) in enumerate(pairs)
        ]

    for group in range(blocks // lanes):
        for copy in copies_of(group):
            copy.start()
    x[:blocks] = even[...]
    x[2 * blocks :] = odd[...]

    def first(b, carry):
        x[blocks + b] = u[b].astype(BF16)
        return carry

    lax.fori_loop(0, blocks, first, 0)
    acc[...] = jnp.zeros_like(acc)

    def emit(b, value):
        term[b] = value
        sent[b] = value.astype(BF16)
        mine = u[b]
        acc[0] += folded(mine * mine)
        acc[1] += folded(mine * (onsite[b] * mine + value))

    def ready(group):
        for copy in copies_of(group):
            copy.wait()

    scalars()
    apply_terms(src, dims, x, left, right, lxs, blocks, terms, width, emit, ready)
    stats[...] = jnp.zeros_like(stats)
    for row in range(2):
        put_row(stats, row, acc[row])


def ahead_kernel(ready, src, dims, even, odd, wave, right, u, y, x):
    blocks, terms, width, _ = right.shape
    x[:blocks] = even[...]
    x[2 * blocks :] = odd[...]
    ready()

    def first(b, carry):
        value = jnp.where(live_of(dims[b], width), wave[b], 0.0)
        u[b] = value
        x[blocks + b] = value.astype(BF16)
        return carry

    lax.fori_loop(0, blocks, first, 0)

    def body(b, carry):
        for k in range(terms):
            part = jnp.dot(x[src[b, k]], right[b, k], preferred_element_type=F32)
            y[b, k * width : (k + 1) * width, :] = part.astype(BF16)
        return carry

    lax.fori_loop(0, blocks, body, 0)


def build_kernel(ready, dims, handed, base, y, u, onsite, term, sent, stats, left, acc, flip, *works):
    blocks, terms, width, _ = base.shape
    lanes = len(works)
    acc[...] = jnp.zeros_like(acc)
    for b in range(blocks):
        flip[b] = (handed[b].astype(F32).T * (1.0 / width)).astype(BF16)
    ready()

    def body(i, carry):
        for j in range(lanes):
            b = i * lanes + j
            work = works[j]
            block = handed[b]
            flipped = flip[b]
            carried = jnp.dot(
                base[b].reshape(terms * width, width), block, preferred_element_type=F32
            )
            work[...] = carried.astype(BF16)
            pieces = []
            for k in range(terms):
                added = jnp.dot(
                    flipped, work[k * width : (k + 1) * width, :], preferred_element_type=F32
                )
                piece = (base[b, k].astype(F32) + added).astype(BF16)
                left[b, k] = piece
                pieces.append(piece)
            total = jnp.dot(jnp.concatenate(pieces, axis=1), y[b], preferred_element_type=F32)
            value = jnp.where(live_of(dims[b], width), total, 0.0)
            term[b] = value
            sent[b] = value.astype(BF16)
            mine = u[b]
            acc[0] += folded(mine * mine)
            acc[1] += folded(mine * (onsite[b] * mine + value))
        return carry

    lax.fori_loop(0, blocks // lanes, body, 0)
    stats[...] = jnp.zeros_like(stats)
    for row in range(2):
        put_row(stats, row, acc[row])


def next_kernel(n_parts, entries, share, first, last, scalars, *refs):
    src, dims, *rest = refs
    parts, rest = rest[:n_parts], rest[n_parts:]
    (u, term, onsite, left, right, u_even, u_odd, t_even, t_odd, w_even, w_odd, *rest) = rest
    if last:
        un, tn, stats, x, acc, *lxs = rest
    else:
        un, tn, sent, stats, un_even, un_odd, x, acc, *lxs = rest
    blocks, width = u.shape[0], u.shape[1]
    terms = left.shape[1]
    sums = totals(parts)
    quotient = sums[1] / sums[0]
    eps = EPS if first else sums[5]
    scale = 1.0 / jnp.sqrt(sums[0] / entries + eps)
    grow = (1.0 + quotient) * scale

    def neighbour(b, w, before, t, kept_at, at):
        value = w[b].astype(F32) * (grow * before[b].astype(F32) - scale * t[b].astype(F32))
        if kept_at is not None:
            kept_at[b] = value
        x[at + b] = value.astype(BF16)

    def move(b, carry):
        neighbour(b, w_even, u_even, t_even, None if last else un_even, 0)
        neighbour(b, w_odd, u_odd, t_odd, None if last else un_odd, 2 * blocks)
        value = (grow * u[b] - scale * term[b]) / (onsite[b] + 1.0)
        un[b] = value
        x[blocks + b] = value.astype(BF16)
        return carry

    lax.fori_loop(0, blocks, move, 0, unroll=2 if blocks % 2 == 0 else 1)
    acc[...] = jnp.zeros_like(acc)

    def emit(b, value):
        tn[b] = value
        mine = un[b]
        acc[0] += folded(mine * mine)
        acc[1] += folded(mine * (onsite[b] * mine + value))
        if last:
            weight = 1.0 / (onsite[b] + 1.0)
            along = weight * mine
            guess = (1.0 + quotient) * along - weight * value
            acc[2] += folded(guess * guess)
            acc[3] += folded(guess * along)
            acc[4] += folded(along * along)
        else:
            sent[b] = value.astype(BF16)

    scalars()
    apply_terms(src, dims, x, left, right, lxs, blocks, terms, width, emit)
    stats[...] = jnp.zeros_like(stats)
    for row in range(5 if last else 2):
        put_row(stats, row, acc[row])
    lanes = stats.shape[1]
    if last:
        stats[5:6, :] = scalar_row(quotient * share, lanes)
    else:
        stats[5:6, :] = scalar_row((EPS * scale * scale if first else EPS) * share, lanes)


def final_kernel(n_parts, entries, *refs):
    parts, rest = refs[:n_parts], refs[n_parts:]
    u, term, onsite, out, *held = rest
    sums = totals(parts)
    quotient = sums[1] / sums[0]
    scale = 1.0 / jnp.sqrt(sums[0] / entries + EPS)
    delta = quotient - sums[5]
    length = sums[2] + 2.0 * delta * sums[3] + delta * delta * sums[4]
    scale = scale / jnp.sqrt(length * scale * scale / entries + EPS)
    grow = (1.0 + quotient) * scale
    blocks = u.shape[0]
    lanes = 2 if blocks % 2 == 0 else 1

    def copy_of(i):
        part = pl.ds(i * lanes, lanes)
        return pltpu.make_async_copy(held[0].at[part], out.at[part], held[1].at[i])

    for i in range(blocks // lanes):
        for b in range(i * lanes, (i + 1) * lanes):
            value = (grow * u[b] - scale * term[b]) / (onsite[b] + 1.0)
            if held:
                held[0][b] = value
            else:
                out[b] = value.astype(out.dtype)
        if held:
            copy_of(i).start()
    if held:
        for i in range(blocks // lanes):
            copy_of(i).wait()


VMEM = pl.BlockSpec(memory_space=pltpu.VMEM)
HBM = pl.BlockSpec(memory_space=pltpu.HBM)


def call(kernel, scalars, arrays, outs, scratch, far=(), out_spec=None):
    count = len(scalars)

    def body(*refs):
        tables, sems = refs[-1 - count : -1], refs[-1]
        copies = [pltpu.make_async_copy(refs[i], tables[i], sems.at[i]) for i in range(count)]
        for copy in copies:
            copy.start()

        def ready():
            for copy in copies:
                copy.wait()

        kernel(ready, *tables, *refs[count : -1 - count])

    held = [pltpu.SMEM(a.shape, a.dtype) for a in scalars]
    held += [pltpu.SemaphoreType.DMA((count,))] if count else []
    return pl.pallas_call(
        body if count else kernel,
        out_shape=outs,
        in_specs=[HBM] * count + [VMEM] * len(arrays) + [HBM] * len(far),
        out_specs=[out_spec or VMEM] * len(outs),
        scratch_shapes=[*scratch, *held],
        compiler_params=pltpu.CompilerParams(vmem_limit_bytes=16 << 20),
    )(
        *[pltpu.with_memory_space_constraint(a, pltpu.HBM) for a in scalars],
        *arrays,
        *[pltpu.with_memory_space_constraint(a, pltpu.HBM) for a in far],
    )


def like(shape, dtype):
    return jax.ShapeDtypeStruct(shape, dtype)


def both_updates(*args):
    (
        wave_first,
        wave_second,
        onsite_first,
        onsite_second,
        left_first,
        right_first,
        left_base,
        right_second,
        sources,
        block_dims,
    ) = [a[0] if a.ndim > 3 else a for a in args]
    blocks, width = wave_first.shape[0], wave_first.shape[1]
    terms = left_first.shape[1]
    count = lax.axis_size("sec")
    entries = float(blocks * count * width * width)

    lanes = max(j for j in (1, 2, 4) if blocks % j == 0)
    vec = (blocks, width, width)
    lxs = [pltpu.VMEM((width, terms * width), BF16)] * lanes
    x_shape = pltpu.VMEM((3 * blocks, width, width), BF16)
    acc_shape = pltpu.VMEM((5, 8, width), F32)
    stats_shape = like((8, width), F32)

    def later_steps(u, term, sent, stats, onsite, left, right, u_halo, w_halo, bundle=None):
        for step in range(1, STEPS):
            last = step == STEPS - 1
            t_halo = swapped(sent)
            parts = gathered_parts(stats)
            if last and bundle is not None:
                arrived = swapped(bundle)
            outs = [like(vec, F32), like(vec, F32)]
            if last:
                outs += [stats_shape]
            else:
                outs += [like(vec, BF16), stats_shape, like(vec, F32), like(vec, F32)]
            res = call(
                functools.partial(
                    next_kernel, len(parts), entries, 1.0 / count, step == 1, last
                ),
                [src, block_dims],
                [*parts, u, term, onsite, left, right, *u_halo, *t_halo, *w_halo],
                outs,
                [x_shape, acc_shape, *lxs],
            )
            if last:
                u, term, stats = res
            else:
                u, term, sent, stats, *u_halo = res
        out = (u, term, gathered_parts(stats))
        return out if bundle is None else (*out, arrived)

    def final(u, term, parts, onsite, narrow):
        held = [] if narrow else [pltpu.VMEM(vec, F32), pltpu.SemaphoreType.DMA((blocks,))]
        (out,) = call(
            functools.partial(final_kernel, len(parts), entries),
            [],
            [*parts, u, term, onsite],
            [like(vec, BF16 if narrow else F32)],
            held,
            (),
            VMEM if narrow else HBM,
        )
        return out

    u, packed = call(
        prepare_kernel,
        [block_dims],
        [],
        [like(vec, F32), like(vec, BF16)],
        [pltpu.SemaphoreType.DMA((blocks,))],
        [wave_first],
    )
    halo_first = swapped(packed)
    weight, bundle = call(
        send_kernel,
        [block_dims],
        [packed],
        [like(vec, BF16), like((2 * blocks, width, width), BF16)],
        [pltpu.VMEM(vec, F32)] * 3 + [pltpu.SemaphoreType.DMA((3,))],
        [onsite_first, onsite_second, wave_second],
    )
    w_first = swapped(weight)
    here = lax.axis_index("sec")
    local = sources - here * blocks + blocks
    group = local // blocks
    src = jnp.where(here % 2 == 0, (2 - group) * blocks + local % blocks, local)

    pairs = max(j for j in (1, 2) if blocks % j == 0)
    term, sent, stats = call(
        start_kernel,
        [src, block_dims],
        [*halo_first, u],
        [like(vec, F32), like(vec, BF16), stats_shape],
        [
            pltpu.VMEM(vec, F32),
            pltpu.VMEM(left_first.shape, BF16),
            pltpu.VMEM(right_first.shape, BF16),
            x_shape,
            acc_shape,
            pltpu.SemaphoreType.DMA((3, blocks // pairs)),
            *lxs[:pairs],
        ],
        [onsite_first, left_first, right_first],
    )
    onsite, left, right = onsite_first, left_first, right_first
    u, term, parts, second = later_steps(
        u, term, sent, stats, onsite, left, right, halo_first, w_first, bundle
    )
    handed = final(u, term, parts, onsite, True)
    ended = (u, term, parts, onsite)
    segs = lax.axis_size("seg")
    handed = lax.ppermute(handed, "seg", [(s, s + 1) for s in range(segs - 1)])

    halo_second = [part[:blocks] for part in second]
    w_second = [part[blocks:] for part in second]
    u, y = call(
        ahead_kernel,
        [src, block_dims],
        [*halo_second, wave_second, right_second],
        [like(vec, F32), like((blocks, terms * width, width), BF16)],
        [x_shape],
    )
    term, sent, stats, left_second = call(
        build_kernel,
        [block_dims],
        [handed, left_base, y, u, onsite_second],
        [like(vec, F32), like(vec, BF16), stats_shape, like(left_base.shape, BF16)],
        [acc_shape, pltpu.VMEM(vec, BF16)] + [pltpu.VMEM((terms * width, width), BF16)] * lanes,
    )
    u_first, term_first, parts_first, onsite = ended
    result_first = final(after(u_first, stats), term_first, parts_first, onsite, False)
    u, term, parts = later_steps(
        u, term, sent, stats, onsite_second, left_second, right_second, halo_second, w_second
    )
    result_second = final(u, term, parts, onsite_second, False)
    return result_first[None], result_second[None]


def solution(mesh):
    vector = P("seg", "sec", None, None)
    matrices = P("seg", "sec", None, None, None)
    placed = (vector,) * 4 + (matrices,) * 4 + (P("sec", None), P("sec"))
    return jax.shard_map(
        both_updates,
        mesh=mesh,
        in_specs=placed,
        out_specs=(vector, vector),
        check_vma=False,
    )
```
